32 devices in a mesh: pair: 8 (over z, x), col: 4 (over y, core).
Axes of the slice: x: 2, y: 2, z: 4, core: 2. Of those that a mesh axis runs over, the one named last changes fastest.
Arguments:
- point_values: bfloat16 [32768, 1024], P('pair', 'col'), may hold values from -2 to 2, as said below
- grid_values: bfloat16 [32768, 512], P('pair'), may hold values from -6 to 6
Outputs:
- fitted: float32 [512, 1024], P(('pair', 'col'))
The draws below stay inside these ranges and needn't reach their ends.
Inputs may be any that keep to these rules, and one draw needn't show every extreme that they name: `point_values`: real pair-product values.
All inputs are finite; a program needn't handle non-finite values.
Results may differ from the reference program's by a relative error of at most 0.0003.
Values may be sent and summed in bfloat16 or wider, within the bound.
A program may use at most 128 MiB of HBM per device.

```python
import math
import jax
import jax.numpy as jnp

NPTS = 1024
PAIRS = 32768
GRID = 512


def draw_point_values(key, part):
    key_noise = jax.random.fold_in(key, 11)
    key_partner = jax.random.fold_in(key, 23)
    key_rows = jax.random.fold_in(key, 37)
    partner = jax.random.permutation(key_partner, NPTS)
    noise_draw = jnp.clip(jax.random.normal(key_noise, (PAIRS, NPTS), jnp.float32), -6.0, 6.0)
    scales = jnp.exp(jax.random.uniform(key_rows, (PAIRS, 1), jnp.float32, 0.0, math.log(4.0)))
    combined = (noise_draw + 0.7 * jnp.take(noise_draw, partner, axis=1)) * scales
    return (combined * (0.35 / math.sqrt(PAIRS))).astype(jnp.bfloat16)


def raised(drawn, stream_key, source, target, parts, factor):
    owner, partner = [(jnp.arange(drawn.shape[axis_at]) // (drawn.shape[axis_at] // parts)).reshape([-1 if axis == axis_at else 1 for axis in range(drawn.ndim)]) for axis_at in (source, target)]
    chosen = jax.random.permutation(stream_key, parts)[partner]
    strong = (owner == chosen) | (owner == (partner + parts // 2) % parts)
    return jnp.where(strong, factor * drawn, drawn)


def levels(key, shape, shards, least, largest):
    loudness, own = 1.0, jax.random.fold_in(key, 6)
    for position, parts in shards:
        draws = jnp.exp(jax.random.uniform(jax.random.fold_in(own, position), (parts,), jnp.float32, least / len(shards), largest / len(shards)))
        loudness = loudness * jnp.repeat(draws, shape[position] // parts).reshape([-1 if axis == position else 1 for axis in range(len(shape))])
    return loudness


def heavy_noise(own_key, extent, spread, reach, cuts, heavy, held_as=jnp.bfloat16):
    entries = spread * jax.random.normal(own_key, extent, jnp.float32)
    if cuts:
        entries = entries * levels(own_key, extent, cuts, -0.22, 0.18)
    return jnp.clip(raised(entries, jax.random.fold_in(own_key, 3), *heavy), -reach, reach).astype(held_as)


def setup_inputs(seed: int = 0) -> dict:
    splits = jax.random.split(jax.random.key(seed), 3)
    return {
        "point_values": draw_point_values(jax.random.fold_in(splits[2], 71), 0),
        "grid_values": heavy_noise(splits[1], (PAIRS, GRID), 1.0, 6.0, ((0, 8),), (0, 1, 8, 2.0)),
    }


def reference(point_values, grid_values):
    gram = jnp.dot(point_values.T.astype(jnp.float32), point_values.astype(jnp.float32), preferred_element_type=jnp.float32)
    factor = jnp.linalg.cholesky(gram)
    project = jnp.dot(grid_values.T.astype(jnp.float32), point_values.astype(jnp.float32), preferred_element_type=jnp.float32)
    solved = jax.scipy.linalg.cho_solve((factor, True), project.T)
    return solved.T
```

```python
import functools

import jax
import jax.numpy as jnp
from jax import lax
from jax.experimental import pallas as pl
from jax.experimental.pallas import tpu as pltpu
from jax.sharding import PartitionSpec as P

NB = 128
TILE = 8
PANEL = 8


def cross(left, right):
    return lax.dot_general(
        left, right, (((0,), (0,)), ((), ())), preferred_element_type=jnp.float32
    )


def dot(left, right):
    return lax.dot_general(
        left, right, (((1,), (0,)), ((), ())),
        precision=lax.Precision.HIGHEST, preferred_element_type=jnp.float32,
    )


def invert(tiles):
    count = len(tiles)
    lane = lax.broadcasted_iota(jnp.int32, (TILE, NB), 1)
    sub = lax.broadcasted_iota(jnp.int32, (TILE, NB), 0)
    for start in range(0, NB, PANEL):
        cols = [
            [jnp.broadcast_to(t[:, start + k : start + k + 1], (TILE, NB)) for t in tiles]
            for k in range(PANEL)
        ]
        for k in range(PANEL):
            j = start + k
            at, s = divmod(j, TILE)
            here, on_row = lane == j, sub == s
            inv = 1.0 / jnp.broadcast_to(cols[k][at][s : s + 1, :], (TILE, NB))
            row = jnp.broadcast_to(tiles[at][s : s + 1, :], (TILE, NB)) * inv
            row = jnp.where(here, inv, row)
            c = list(cols[k])
            c[at] = jnp.where(on_row, -1.0, c[at])
            for m in range(k + 1, PANEL):
                r = jnp.broadcast_to(cols[m][at][s : s + 1, :], (TILE, NB)) * inv
                old = list(cols[m])
                old[at] = jnp.where(on_row, 0.0, old[at])
                cols[m] = [old[i] - c[i] * r for i in range(count)]
            old = [jnp.where(here, 0.0, t) for t in tiles]
            old[at] = jnp.where(on_row, 0.0, old[at])
            tiles = [old[i] - c[i] * row for i in range(count)]
    return tiles


def solve_kernel(cols, gram_ref, rhs_ref, out_ref, work, inverse):
    n = work.shape[1]
    rows = rhs_ref.shape[0]
    blocks = n // NB
    width = n // cols
    for i in range(gram_ref.shape[0]):
        p, c = divmod(i, cols)
        height = gram_ref.shape[1]
        work[p * height : (p + 1) * height, c * width : (c + 1) * width] = gram_ref[i]
    work[n : n + rows, :] = rhs_ref[...]

    def step(k, carry):
        for kk in range(blocks):
            @pl.when(k == kk)
            def _():
                inverse[...] = work[kk * NB : (kk + 1) * NB, kk * NB : (kk + 1) * NB]

        tiles = invert([inverse[i : i + TILE, :] for i in range(0, NB, TILE)])
        for i, t in enumerate(tiles):
            inverse[i * TILE : (i + 1) * TILE, :] = t

        for kk in range(blocks):
            @pl.when(k == kk)
            def _():
                lo, hi = kk * NB, (kk + 1) * NB
                scaled = dot(work[hi : n + rows, lo:hi], inverse[...])
                work[hi : n + rows, lo:hi] = scaled
                if hi < n:
                    work[hi : n + rows, hi:n] -= dot(scaled, work[lo:hi, hi:n])
        return carry

    lax.fori_loop(0, blocks, step, 0)
    for kk in range(blocks - 1, -1, -1):
        lo, hi = kk * NB, (kk + 1) * NB
        x = work[n : n + rows, lo:hi]
        if hi < n:
            x = x - dot(out_ref[:, hi:n], work[hi:n, lo:hi])
        out_ref[:, lo:hi] = x


def solve(gram_parts, rhs, cols):
    rows, n = rhs.shape
    vmem = pl.BlockSpec(memory_space=pltpu.VMEM)
    return pl.pallas_call(
        functools.partial(solve_kernel, cols),
        out_shape=jax.ShapeDtypeStruct((rows, n), jnp.float32),
        in_specs=[vmem, vmem],
        out_specs=vmem,
        scratch_shapes=[
            pltpu.VMEM((n + rows, n), jnp.float32),
            pltpu.VMEM((NB, NB), jnp.float32),
        ],
        compiler_params=pltpu.CompilerParams(vmem_limit_bytes=48 << 20),
    )(gram_parts, rhs)


def solution(mesh):
    cols = mesh.shape["col"]

    def body(point_values, grid_values):
        gathered = lax.all_gather(point_values, "col", axis=1, tiled=True)
        gram = lax.psum_scatter(
            cross(gathered, point_values), "pair", scatter_dimension=0, tiled=True
        )
        gram_parts = lax.all_gather(gram, ("pair", "col"), axis=0, tiled=False)
        summed = lax.psum_scatter(
            cross(grid_values, point_values), "pair", scatter_dimension=0, tiled=True
        )
        regrouped = lax.all_to_all(summed, "col", split_axis=0, concat_axis=1, tiled=True)
        return solve(gram_parts, regrouped, cols)

    in_specs = (P("pair", "col"), P("pair", None))
    out_specs = P(("pair", "col"), None)
    return jax.shard_map(body, mesh=mesh, in_specs=in_specs, out_specs=out_specs, check_vma=False)
```

```python
import functools

import jax
import jax.numpy as jnp
from jax import lax
from jax.experimental import pallas as pl
from jax.experimental.pallas import tpu as pltpu
from jax.sharding import PartitionSpec as P

NB = 128
TILE = 8
PANEL = 8


def cross(left, right):
    return lax.dot_general(
        left, right, (((0,), (0,)), ((), ())), preferred_element_type=jnp.float32
    )


def dot(left, right):
    return lax.dot_general(
        left, right, (((1,), (0,)), ((), ())),
        precision=lax.Precision.HIGHEST, preferred_element_type=jnp.float32,
    )


def invert(tiles):
    count = len(tiles)
    lane = lax.broadcasted_iota(jnp.int32, (TILE, NB), 1)
    sub = lax.broadcasted_iota(jnp.int32, (TILE, NB), 0)
    for start in range(0, NB, PANEL):
        cols = [
            [jnp.broadcast_to(t[:, start + k : start + k + 1], (TILE, NB)) for t in tiles]
            for k in range(PANEL)
        ]
        for k in range(PANEL):
            j = start + k
            at, s = divmod(j, TILE)
            here, on_row = lane == j, sub == s
            inv = 1.0 / jnp.broadcast_to(cols[k][at][s : s + 1, :], (TILE, NB))
            row = jnp.broadcast_to(tiles[at][s : s + 1, :], (TILE, NB)) * inv
            row = jnp.where(here, inv, row)
            c = list(cols[k])
            c[at] = jnp.where(on_row, -1.0, c[at])
            for m in range(k + 1, PANEL):
                r = jnp.broadcast_to(cols[m][at][s : s + 1, :], (TILE, NB)) * inv
                old = list(cols[m])
                old[at] = jnp.where(on_row, 0.0, old[at])
                cols[m] = [old[i] - c[i] * r for i in range(count)]
            old = [jnp.where(here, 0.0, t) for t in tiles]
            old[at] = jnp.where(on_row, 0.0, old[at])
            tiles = [old[i] - c[i] * row for i in range(count)]
    return tiles


def solve_kernel(cols, folded, gram_ref, rhs_ref, out_ref, work, inverse):
    n = work.shape[1]
    rows = rhs_ref.shape[0]
    blocks = n // NB
    width = n // cols
    height = gram_ref.shape[1]
    for i in range(gram_ref.shape[0]):
        p, c = divmod(i, cols)
        part, at = divmod(p * height, width)
        if not folded or part < 2:
            block = c ^ part if folded else part
            top = block * width + at
            work[top : top + height, c * width : (c + 1) * width] = gram_ref[i]
    if folded:
        def part_of(part, c):
            first = part * width // height
            return jnp.concatenate(
                [gram_ref[(first + h) * cols + c] for h in range(width // height)], axis=0
            )
        for part in (2, 3):
            for c in range(2):
                row, col = c ^ 2, c ^ (part - 2)
                total = part_of(part, c) + part_of(part, c ^ part).T
                work[row * width : (row + 1) * width, col * width : (col + 1) * width] = total
                work[col * width : (col + 1) * width, row * width : (row + 1) * width] = total.T
    work[n : n + rows, :] = rhs_ref[...]

    def step(k, carry):
        for kk in range(blocks):
            @pl.when(k == kk)
            def _():
                inverse[...] = work[kk * NB : (kk + 1) * NB, kk * NB : (kk + 1) * NB]

        tiles = invert([inverse[i : i + TILE, :] for i in range(0, NB, TILE)])
        for i, t in enumerate(tiles):
            inverse[i * TILE : (i + 1) * TILE, :] = t

        for kk in range(blocks):
            @pl.when(k == kk)
            def _():
                lo, hi = kk * NB, (kk + 1) * NB
                scaled = dot(work[hi : n + rows, lo:hi], inverse[...])
                work[hi : n + rows, lo:hi] = scaled
                if hi < n:
                    work[hi : n + rows, hi:n] -= dot(scaled, work[lo:hi, hi:n])
        return carry

    lax.fori_loop(0, blocks, step, 0)
    for kk in range(blocks - 1, -1, -1):
        lo, hi = kk * NB, (kk + 1) * NB
        x = work[n : n + rows, lo:hi]
        if hi < n:
            x = x - dot(out_ref[:, hi:n], work[hi:n, lo:hi])
        out_ref[:, lo:hi] = x


def solve(gram_parts, rhs, cols, folded):
    rows, n = rhs.shape
    vmem = pl.BlockSpec(memory_space=pltpu.VMEM)
    return pl.pallas_call(
        functools.partial(solve_kernel, cols, folded),
        out_shape=jax.ShapeDtypeStruct((rows, n), jnp.float32),
        in_specs=[vmem, vmem],
        out_specs=vmem,
        scratch_shapes=[
            pltpu.VMEM((n + rows, n), jnp.float32),
            pltpu.VMEM((NB, NB), jnp.float32),
        ],
        compiler_params=pltpu.CompilerParams(vmem_limit_bytes=48 << 20),
    )(gram_parts, rhs)


def fold(own):
    c = lax.axis_index("col")
    half = own.shape[0] // 2
    y = c // 2
    other = lax.dynamic_slice_in_dim(own, (1 - y) * half, half, 0)
    received = lax.ppermute(other, "col", [(i, i ^ 2) for i in range(4)])
    sibling = lax.ppermute(own, "col", [(i, i ^ 1) for i in range(4)])
    own_half = lax.dynamic_slice_in_dim(own, y * half, half, 0)
    sibling_half = lax.dynamic_slice_in_dim(sibling, y * half, half, 0)
    return jnp.concatenate(
        [cross(own, own), cross(sibling, own), cross(received, own_half), cross(received, sibling_half)],
        axis=0,
    )


def solution(mesh):
    cols, pairs = mesh.shape["col"], mesh.shape["pair"]
    folded = cols == 4

    def body(point_values, grid_values):
        project = cross(grid_values, point_values)
        if folded:
            gram = fold(point_values)
        else:
            gathered = lax.all_gather(point_values, "col", axis=1, tiled=True)
            gram = cross(gathered, point_values)
        width = gram.shape[1]
        both = jnp.concatenate(
            [gram.reshape(pairs, -1, width), project.reshape(pairs, -1, width)], axis=1
        )
        own = lax.psum_scatter(both, "pair", scatter_dimension=0, tiled=False)
        height = gram.shape[0] // pairs
        gram_parts = lax.all_gather(own[:height], ("pair", "col"), axis=0, tiled=False)
        regrouped = lax.all_to_all(own[height:], "col", split_axis=0, concat_axis=1, tiled=True)
        return solve(gram_parts, regrouped, cols, folded)

    in_specs = (P("pair", "col"), P("pair", None))
    out_specs = P(("pair", "col"), None)
    return jax.shard_map(body, mesh=mesh, in_specs=in_specs, out_specs=out_specs, check_vma=False)
```

```python
import functools

import jax
import jax.numpy as jnp
from jax import lax
from jax.experimental import pallas as pl
from jax.experimental.pallas import tpu as pltpu
from jax.sharding import PartitionSpec as P

NB = 128
TILE = 8
PANEL = 8


def cross(left, right):
    return lax.dot_general(
        left, right, (((0,), (0,)), ((), ())), preferred_element_type=jnp.float32
    )


def dot(left, right):
    return lax.dot_general(
        left, right, (((1,), (0,)), ((), ())),
        precision=lax.Precision.HIGHEST, preferred_element_type=jnp.float32,
    )


def invert(tiles):
    count = len(tiles)
    lane = lax.broadcasted_iota(jnp.int32, (TILE, NB), 1)
    sub = lax.broadcasted_iota(jnp.int32, (TILE, NB), 0)
    for start in range(0, NB, PANEL):
        cols = [
            [jnp.broadcast_to(t[:, start + k : start + k + 1], (TILE, NB)) for t in tiles]
            for k in range(PANEL)
        ]
        for k in range(PANEL):
            j = start + k
            at, s = divmod(j, TILE)
            here, on_row = lane == j, sub == s
            inv = 1.0 / jnp.broadcast_to(cols[k][at][s : s + 1, :], (TILE, NB))
            row = jnp.broadcast_to(tiles[at][s : s + 1, :], (TILE, NB)) * inv
            row = jnp.where(here, inv, row)
            c = list(cols[k])
            c[at] = jnp.where(on_row, -1.0, c[at])
            for m in range(k + 1, PANEL):
                r = jnp.broadcast_to(cols[m][at][s : s + 1, :], (TILE, NB)) * inv
                old = list(cols[m])
                old[at] = jnp.where(on_row, 0.0, old[at])
                cols[m] = [old[i] - c[i] * r for i in range(count)]
            old = [jnp.where(here, 0.0, t) for t in tiles]
            old[at] = jnp.where(on_row, 0.0, old[at])
            tiles = [old[i] - c[i] * row for i in range(count)]
    return tiles


def solve_kernel(cols, folded, gram_ref, rhs_ref, out_ref, work, inverse):
    n = work.shape[1]
    rows = rhs_ref.shape[0]
    blocks = n // NB
    width = n // cols
    height = gram_ref.shape[1]
    for i in range(gram_ref.shape[0]):
        p, c = divmod(i, cols)
        part, at = divmod(p * height, width)
        if not folded or part < 2:
            block = c ^ part if folded else part
            top = block * width + at
            work[top : top + height, c * width : (c + 1) * width] = gram_ref[i]
    if folded:
        def part_of(part, c):
            first = part * width // height
            return jnp.concatenate(
                [gram_ref[(first + h) * cols + c] for h in range(width // height)], axis=0
            )
        for part in (2, 3):
            for c in range(2):
                row, col = c ^ 2, c ^ (part - 2)
                total = part_of(part, c) + part_of(part, c ^ part).T
                work[row * width : (row + 1) * width, col * width : (col + 1) * width] = total
                work[col * width : (col + 1) * width, row * width : (row + 1) * width] = total.T
    work[n : n + rows, :] = rhs_ref[...]

    def step(k, carry):
        for kk in range(blocks):
            @pl.when(k == kk)
            def _():
                inverse[...] = work[kk * NB : (kk + 1) * NB, kk * NB : (kk + 1) * NB]

        tiles = invert([inverse[i : i + TILE, :] for i in range(0, NB, TILE)])
        for i, t in enumerate(tiles):
            inverse[i * TILE : (i + 1) * TILE, :] = t

        for kk in range(blocks):
            @pl.when(k == kk)
            def _():
                lo, hi = kk * NB, (kk + 1) * NB
                scaled = dot(work[hi : n + rows, lo:hi], inverse[...])
                work[hi : n + rows, lo:hi] = scaled
                if hi < n:
                    work[hi : n + rows, hi:n] -= dot(scaled, work[lo:hi, hi:n])
        return carry

    lax.fori_loop(0, blocks, step, 0)
    for kk in range(blocks - 1, -1, -1):
        lo, hi = kk * NB, (kk + 1) * NB
        x = work[n : n + rows, lo:hi]
        if hi < n:
            x = x - dot(out_ref[:, hi:n], work[hi:n, lo:hi])
        out_ref[:, lo:hi] = x


def solve(gram_parts, rhs, cols, folded):
    rows, n = rhs.shape
    vmem = pl.BlockSpec(memory_space=pltpu.VMEM)
    return pl.pallas_call(
        functools.partial(solve_kernel, cols, folded),
        out_shape=jax.ShapeDtypeStruct((rows, n), jnp.float32),
        in_specs=[vmem, vmem],
        out_specs=vmem,
        scratch_shapes=[
            pltpu.VMEM((n + rows, n), jnp.float32),
            pltpu.VMEM((NB, NB), jnp.float32),
        ],
        compiler_params=pltpu.CompilerParams(vmem_limit_bytes=48 << 20),
    )(gram_parts, rhs)


def fold(own):
    c = lax.axis_index("col")
    half = own.shape[0] // 2
    y = c // 2
    other = lax.dynamic_slice_in_dim(own, (1 - y) * half, half, 0)
    received = lax.ppermute(other, "col", [(i, i ^ 2) for i in range(4)])
    sibling = lax.ppermute(own, "col", [(i, i ^ 1) for i in range(4)])
    own_half = lax.dynamic_slice_in_dim(own, y * half, half, 0)
    sibling_half = lax.dynamic_slice_in_dim(sibling, y * half, half, 0)
    return jnp.concatenate(
        [cross(own, own), cross(sibling, own), cross(received, own_half), cross(received, sibling_half)],
        axis=0,
    )


def solution(mesh):
    cols, pairs = mesh.shape["col"], mesh.shape["pair"]
    folded = cols == 4

    def body(point_values, grid_values):
        project = cross(grid_values, point_values)
        if folded:
            gram = fold(point_values)
        else:
            gathered = lax.all_gather(point_values, "col", axis=1, tiled=True)
            gram = cross(gathered, point_values)
        width = gram.shape[1]
        both = jnp.concatenate(
            [gram.reshape(pairs, -1, width), project.reshape(pairs, -1, width)], axis=1
        )
        exchanged = lax.all_to_all(both, "pair", split_axis=0, concat_axis=0, tiled=True)
        own = jnp.sum(exchanged, axis=0)
        height = gram.shape[0] // pairs
        gram_parts = lax.all_gather(own[:height], ("pair", "col"), axis=0, tiled=False)
        regrouped = lax.all_to_all(own[height:], "col", split_axis=0, concat_axis=1, tiled=True)
        return solve(gram_parts, regrouped, cols, folded)

    in_specs = (P("pair", "col"), P("pair", None))
    out_specs = P(("pair", "col"), None)
    return jax.shard_map(body, mesh=mesh, in_specs=in_specs, out_specs=out_specs, check_vma=False)
```

```python
import functools

import jax
import jax.numpy as jnp
from jax import lax
from jax.experimental import pallas as pl
from jax.experimental.pallas import tpu as pltpu
from jax.sharding import PartitionSpec as P

NB = 128
TILE = 8
PANEL = 8


def cross(left, right):
    return lax.dot_general(
        left, right, (((0,), (0,)), ((), ())), preferred_element_type=jnp.float32
    )


def dot(left, right):
    return lax.dot_general(
        left, right, (((1,), (0,)), ((), ())),
        precision=lax.Precision.HIGHEST, preferred_element_type=jnp.float32,
    )


def invert(tiles):
    count = len(tiles)
    lane = lax.broadcasted_iota(jnp.int32, (TILE, NB), 1)
    sub = lax.broadcasted_iota(jnp.int32, (TILE, NB), 0)
    for start in range(0, NB, PANEL):
        cols = [
            [jnp.broadcast_to(t[:, start + k : start + k + 1], (TILE, NB)) for t in tiles]
            for k in range(PANEL)
        ]
        for k in range(PANEL):
            j = start + k
            at, s = divmod(j, TILE)
            here, on_row = lane == j, sub == s
            inv = 1.0 / jnp.broadcast_to(cols[k][at][s : s + 1, :], (TILE, NB))
            row = jnp.broadcast_to(tiles[at][s : s + 1, :], (TILE, NB)) * inv
            row = jnp.where(here, inv, row)
            c = list(cols[k])
            c[at] = jnp.where(on_row, -1.0, c[at])
            for m in range(k + 1, PANEL):
                r = jnp.broadcast_to(cols[m][at][s : s + 1, :], (TILE, NB)) * inv
                old = list(cols[m])
                old[at] = jnp.where(on_row, 0.0, old[at])
                cols[m] = [old[i] - c[i] * r for i in range(count)]
            old = [jnp.where(here, 0.0, t) for t in tiles]
            old[at] = jnp.where(on_row, 0.0, old[at])
            tiles = [old[i] - c[i] * row for i in range(count)]
    return tiles


def solve_kernel(cols, folded, gram_ref, rhs_ref, out_ref, work, inverse):
    n = work.shape[1]
    rows = rhs_ref.shape[0]
    blocks = n // NB
    width = n // cols
    height = gram_ref.shape[1]
    if folded:
        half = width // 2
        quarter = half // 2

        def put(row, col, block):
            h, w = block.shape
            work[row : row + h, col : col + w] = block

        held = []
        for c in range(cols):
            held.append(jnp.concatenate(
                [gram_ref[p * cols + c] for p in range(gram_ref.shape[0] // cols)], axis=0
            ))
        cross_at = half + quarter + half
        for c in range(cols):
            at = c * width
            low = held[c][:half]
            corner = held[c][half : half + quarter]
            put(at + half, at, low)
            put(at, at + half, low[:, :half].T)
            put(at, at, corner[:, :half])
            put(at + quarter, at, corner[:, half:])
        for c in (0, 2):
            both = jnp.concatenate(
                [held[c + core][half + quarter : cross_at] for core in range(2)], axis=0
            )
            put(c * width, (c + 1) * width, both)
            put((c + 1) * width, c * width, both.T)
        for part in (2, 3):
            first = cross_at + (part - 2) * width
            for c in range(2):
                row, col = c ^ 2, c ^ (part - 2)
                total = held[c][first : first + width] + held[c ^ part][first : first + width].T
                put(row * width, col * width, total)
                put(col * width, row * width, total.T)
    else:
        for i in range(gram_ref.shape[0]):
            p, c = divmod(i, cols)
            work[p * height : (p + 1) * height, c * width : (c + 1) * width] = gram_ref[i]
    work[n : n + rows, :] = rhs_ref[...]

    def step(k, carry):
        for kk in range(blocks):
            @pl.when(k == kk)
            def _():
                inverse[...] = work[kk * NB : (kk + 1) * NB, kk * NB : (kk + 1) * NB]

        tiles = invert([inverse[i : i + TILE, :] for i in range(0, NB, TILE)])
        for i, t in enumerate(tiles):
            inverse[i * TILE : (i + 1) * TILE, :] = t

        for kk in range(blocks):
            @pl.when(k == kk)
            def _():
                lo, hi = kk * NB, (kk + 1) * NB
                scaled = dot(work[hi : n + rows, lo:hi], inverse[...])
                work[hi : n + rows, lo:hi] = scaled
                if hi < n:
                    work[hi : n + rows, hi:n] -= dot(scaled, work[lo:hi, hi:n])
        return carry

    lax.fori_loop(0, blocks, step, 0)
    for kk in range(blocks - 1, -1, -1):
        lo, hi = kk * NB, (kk + 1) * NB
        x = work[n : n + rows, lo:hi]
        if hi < n:
            x = x - dot(out_ref[:, hi:n], work[hi:n, lo:hi])
        out_ref[:, lo:hi] = x


def solve(gram_parts, rhs, cols, folded):
    rows, n = rhs.shape
    vmem = pl.BlockSpec(memory_space=pltpu.VMEM)
    return pl.pallas_call(
        functools.partial(solve_kernel, cols, folded),
        out_shape=jax.ShapeDtypeStruct((rows, n), jnp.float32),
        in_specs=[vmem, vmem],
        out_specs=vmem,
        scratch_shapes=[
            pltpu.VMEM((n + rows, n), jnp.float32),
            pltpu.VMEM((NB, NB), jnp.float32),
        ],
        compiler_params=pltpu.CompilerParams(vmem_limit_bytes=48 << 20),
    )(gram_parts, rhs)


def fold(own):
    c = lax.axis_index("col")
    half = own.shape[0] // 2
    y = c // 2
    other = lax.dynamic_slice_in_dim(own, (1 - y) * half, half, 0)
    received = lax.ppermute(other, "col", [(i, i ^ 2) for i in range(4)])
    sibling = lax.ppermute(own, "col", [(i, i ^ 1) for i in range(4)])
    own_half = lax.dynamic_slice_in_dim(own, y * half, half, 0)
    sibling_half = lax.dynamic_slice_in_dim(sibling, y * half, half, 0)
    square = cross(own, own)
    width = square.shape[0]
    mid = width // 2
    corner = square[:mid, :mid]
    corner = jnp.concatenate([corner[: mid // 2], corner[mid // 2 :]], axis=1)
    beside = cross(sibling, own)
    beside = jnp.where(c % 2 == 0, beside.T[:mid], beside[mid:])
    return jnp.concatenate(
        [square[mid:], corner, beside, cross(received, own_half), cross(received, sibling_half)],
        axis=0,
    )


def solution(mesh):
    cols, pairs = mesh.shape["col"], mesh.shape["pair"]
    folded = cols == 4 and pairs == 8

    def body(point_values, grid_values):
        project = cross(grid_values, point_values)
        if folded:
            gram = fold(point_values)
        else:
            gathered = lax.all_gather(point_values, "col", axis=1, tiled=True)
            gram = cross(gathered, point_values)
        width = gram.shape[1]
        both = jnp.concatenate(
            [gram.reshape(pairs, -1, width), project.reshape(pairs, -1, width)], axis=1
        )
        exchanged = lax.all_to_all(both, "pair", split_axis=0, concat_axis=0, tiled=True)
        own = jnp.sum(exchanged, axis=0)
        height = gram.shape[0] // pairs
        gram_parts = lax.all_gather(own[:height], ("pair", "col"), axis=0, tiled=False)
        regrouped = lax.all_to_all(own[height:], "col", split_axis=0, concat_axis=1, tiled=True)
        return solve(gram_parts, regrouped, cols, folded)

    in_specs = (P("pair", "col"), P("pair", None))
    out_specs = P(("pair", "col"), None)
    return jax.shard_map(body, mesh=mesh, in_specs=in_specs, out_specs=out_specs, check_vma=False)
```
